32 devices in a mesh: tmpl: 2 (over core), row: 16 (over z, y, x).
Axes of the slice: x: 2, y: 2, z: 4, core: 2. Of those that a mesh axis runs over, the one named last changes fastest.
Arguments:
- pair_maps: bfloat16 [2, 2048, 2048, 64], P('tmpl', 'row'), may hold values from -6 to 6
- crop_tiles: int32 [2, 8], P('tmpl'), may hold values from 0 to 15, as said below
- full_length: int32 [1], replicated, may hold values from 1536 to 2048
- proj_weight: bfloat16 [2, 64, 320], replicated, may hold values from -0.75 to 0.75
- out_weight: bfloat16 [2, 64, 64], replicated, may hold values from -0.75 to 0.75
- final_weight: bfloat16 [64, 128], replicated, may hold values from -0.75 to 0.75
Outputs:
- embedding: bfloat16 [128, 1024, 1024], P(None, 'row')
The draws below stay inside these ranges and needn't reach their ends.
Inputs may be any that keep to these rules, and one draw needn't show every extreme that they name: Each row of crop_tiles names 8 different tiles of the 16, in increasing order; its last 4 entries are the tiles 16 - 8 // 2 to 15.
All inputs are finite; a program needn't handle non-finite values.
Results may differ from the reference program's by a relative error of at most 0.014.
Values may be sent and summed in bfloat16 or wider, within the bound.
A program may use at most 256 MiB of HBM per device.

```python
import jax
import jax.numpy as jnp
from jax import lax

CH = 64
CZ = 128
CROP = 1024
TILE = 128
NLAYER = 2
FULL = 2048
TEMPLATES = 2
NTILES = 16
NCROP = 8


def draw_crop_tiles(key, part):
    keys = jax.random.split(jax.random.fold_in(key, 17), TEMPLATES)
    tail_count = NCROP // 2
    head_pool = NTILES - tail_count
    tail_tiles = (jnp.arange(tail_count, dtype=jnp.int32) + head_pool).astype(jnp.int32)

    def one_template(single_key):
        order = jax.random.permutation(single_key, head_pool)
        head_tiles = jnp.sort(order[:NCROP - tail_count]).astype(jnp.int32)
        return jnp.concatenate([head_tiles, tail_tiles]).astype(jnp.int32)
    return jax.vmap(one_template)(keys)


def shard_levels(key, dims, cuts, smallest, top_value):
    gain, own = 1.0, jax.random.fold_in(key, 6)
    for dim, shards_of in cuts:
        steps = jnp.exp(jax.random.uniform(jax.random.fold_in(own, dim), (shards_of,), jnp.float32, smallest / len(cuts), top_value / len(cuts)))
        gain = gain * jnp.repeat(steps, dims[dim] // shards_of).reshape([-1 if axis == dim else 1 for axis in range(len(dims))])
    return gain


def gaussian(rng, dims, scale, bound, cuts=(), held_as=jnp.bfloat16):
    values = jax.random.normal(rng, dims, jnp.float32) * scale
    if len(cuts) > 0:
        values = shard_levels(rng, dims, cuts, -0.22, 0.18) * values
    return jnp.clip(values, min=-bound, max=bound).astype(held_as)


def setup_inputs(seed: int = 0) -> dict:
    streams_of = jax.random.split(jax.random.key(seed), 7)
    pair_maps = gaussian(streams_of[0], (TEMPLATES, FULL, FULL, CH), 1.0, 6.0, ((0, 2), (1, 16)))
    crop_tiles = draw_crop_tiles(jax.random.fold_in(streams_of[6], 71), 0)
    full_length = jax.random.randint(streams_of[2], (1,), FULL - CROP // 2, FULL + 1).astype(jnp.int32)
    proj_weight = gaussian(streams_of[3], (NLAYER, CH, 5 * CH), CH ** -0.5, 0.75)
    out_weight = gaussian(streams_of[4], (NLAYER, CH, CH), CH ** -0.5, 0.75)
    final_weight = gaussian(streams_of[5], (CH, CZ), CH ** -0.5, 0.75)
    return {"pair_maps": pair_maps, "crop_tiles": crop_tiles, "full_length": full_length, "proj_weight": proj_weight, "out_weight": out_weight, "final_weight": final_weight}


EPSILON = 1e-05

def channel_norm(values, axis_pos):
    center = values - lax.optimization_barrier(jnp.mean(values, axis=axis_pos, keepdims=True))
    spread = lax.optimization_barrier(jnp.mean(center * center, axis=axis_pos, keepdims=True))
    return center * lax.rsqrt(spread + EPSILON)

def outgoing_layer(current, usable, w_proj, w_out):
    normed_in = channel_norm(current.astype(jnp.float32), -1).astype(jnp.bfloat16)
    projected = jnp.dot(normed_in.reshape(-1, CH), w_proj, preferred_element_type=jnp.float32).reshape(CROP, CROP, 5 * CH)
    pair_mask = (usable[:, None] * usable[None, :])[:, :, None]
    left_proj = (jax.nn.sigmoid(projected[..., :CH]) * projected[..., CH:2 * CH] * pair_mask).astype(jnp.bfloat16)
    right_proj = (jax.nn.sigmoid(projected[..., 2 * CH:3 * CH]) * projected[..., 3 * CH:4 * CH] * pair_mask).astype(jnp.bfloat16)
    gate_vals = jax.nn.sigmoid(projected[..., 4 * CH:])
    left_first = jnp.transpose(left_proj, (2, 0, 1)).astype(jnp.float32)
    right_first = jnp.transpose(right_proj, (2, 0, 1)).astype(jnp.float32)
    products = jnp.einsum('cik,cjk->cij', left_first, right_first).astype(jnp.bfloat16)
    products = jnp.transpose(products, (1, 2, 0))
    normed_out = channel_norm(products.astype(jnp.float32), -1).astype(jnp.bfloat16)
    update = jnp.dot(normed_out.reshape(-1, CH), w_out, preferred_element_type=jnp.float32).reshape(CROP, CROP, CH)
    return (current.astype(jnp.float32) + gate_vals * update).astype(jnp.bfloat16)

def reference(pair_maps, crop_tiles, full_length, proj_weight, out_weight, final_weight):
    total = jnp.zeros((CROP, CROP, CH), jnp.float32)
    steps_crop = jnp.arange(CROP, dtype=jnp.int32)
    for template_idx in range(TEMPLATES):
        crop_ids = crop_tiles[template_idx].astype(jnp.int32)
        position = crop_ids[steps_crop // TILE] * TILE + steps_crop % TILE
        usable = (position < full_length[0]).astype(jnp.float32)
        full_map = pair_maps[template_idx].reshape(NTILES, TILE, FULL, CH)[crop_ids]
        full_map = full_map.reshape(CROP, NTILES, TILE, CH)[:, crop_ids]
        current = full_map.reshape(CROP, CROP, CH)
        for layer_idx in range(NLAYER):
            current = outgoing_layer(current, usable, proj_weight[layer_idx], out_weight[layer_idx])
        total = total + channel_norm(current.astype(jnp.float32), -1)
    mean_pair = total / TEMPLATES
    hidden = jnp.maximum(mean_pair, 0.0).astype(jnp.bfloat16)
    result = jnp.dot(hidden.reshape(-1, CH), final_weight, preferred_element_type=jnp.float32).reshape(CROP, CROP, CZ)
    return jnp.transpose(result, (2, 1, 0)).astype(jnp.bfloat16)
```

```python
import jax
import jax.numpy as jnp
from jax import lax
from jax.experimental import pallas as pl
from jax.experimental.pallas import tpu as pltpu
from jax.sharding import PartitionSpec as P

CH = 64
CROP = 1024
TILE = 128
NLAYER = 2
FULL = 2048


EPSILON = 1e-05


def from_partner(value, axis, bit):
    mask = 2**bit
    pairs = [(source, source ^ mask) for source in range(lax.axis_size(axis))]
    return lax.ppermute(value, axis, pairs)


def channel_norm(values):
    center = values - jnp.mean(values, axis=0, keepdims=True)
    spread = jnp.mean(center * center, axis=0, keepdims=True)
    return center * lax.rsqrt(spread + EPSILON)


SPLIT = 2


def product_kernel(left_ref, *refs):
    rights, out_ref = refs[:-1], refs[-1]
    sources, _, width, chunk = left_ref.shape
    left = left_ref[...].reshape(sources * width, chunk)
    per = out_ref.shape[0] // len(rights)
    for number, right_ref in enumerate(rights):
        right = right_ref[...].reshape(sources * width, right_ref.shape[-1])
        product = lax.dot_general(
            right, left, (((0,), (0,)), ((), ())), preferred_element_type=jnp.float32
        )
        out_ref[number * per : (number + 1) * per] = product.astype(out_ref.dtype).reshape(
            per, 1, width, chunk
        )


def channel_products(left, rights):
    sources, channels, width, chunk = left.shape
    spec = pl.BlockSpec((sources, 1, width, chunk), lambda c: (0, c, 0, 0))
    depth = sources * width
    return pl.pallas_call(
        product_kernel,
        grid=(channels,),
        in_specs=[spec] * (1 + len(rights)),
        out_specs=spec,
        out_shape=jax.ShapeDtypeStruct(left.shape, left.dtype),
        compiler_params=pltpu.CompilerParams(vmem_limit_bytes=32 << 20),
        cost_estimate=pl.CostEstimate(
            flops=2 * channels * depth * depth * chunk,
            bytes_accessed=2 * left.size * (2 + len(rights)),
            transcendentals=0,
        ),
    )(left, *rights)


def exchange(value):
    return lax.all_to_all(value, "row", split_axis=0, concat_axis=0, tiled=True)


def in_chunks(pair_maps, crop_tiles, full_length, proj_weight, out_weight, final_weight):
    row_count = lax.axis_size("row")
    my_index = lax.axis_index("row")
    crop_ids = crop_tiles[0]
    col_width = CROP // row_count
    per_group = CH // row_count
    tiles = CROP // TILE
    chunk = CROP // SPLIT
    steps_crop = jnp.arange(CROP, dtype=jnp.int32)
    position = crop_ids[steps_crop // TILE] * TILE + steps_crop % TILE
    usable = (position < full_length[0]).astype(jnp.float32)
    col_usable = lax.dynamic_slice_in_dim(usable, my_index * col_width, col_width)
    pair_mask = col_usable[:, None] * usable[None, :]
    masks = jnp.split(pair_mask, SPLIT, axis=1)
    by_channel = jnp.transpose(pair_maps[0], (0, 2, 1))
    columns = jnp.concatenate(
        [
            lax.dynamic_slice_in_dim(by_channel, crop_ids[tile] * TILE, TILE, axis=2)
            for tile in range(tiles)
        ],
        axis=2,
    )
    send = jnp.transpose(columns, (2, 1, 0)).reshape(row_count, col_width, CH, TILE)
    got = exchange(send)
    per = tiles // SPLIT
    current = []
    for number in range(SPLIT):
        pieces = [
            lax.dynamic_index_in_dim(got, crop_ids[number * per + tile], 0, keepdims=False)
            for tile in range(per)
        ]
        current.append(jnp.transpose(jnp.concatenate(pieces, axis=2), (1, 0, 2)))
    for layer_idx in range(NLAYER):
        lefts, rights, gates = [], [], []
        for values, mask in zip(current, masks):
            normed_in = channel_norm(values.astype(jnp.float32)).astype(jnp.bfloat16)
            projected = jnp.einsum(
                "cd,cwi->dwi", proj_weight[layer_idx], normed_in, preferred_element_type=jnp.float32
            )
            left = jax.nn.sigmoid(projected[:CH]) * projected[CH : 2 * CH] * mask
            right = jax.nn.sigmoid(projected[2 * CH : 3 * CH]) * projected[3 * CH : 4 * CH] * mask
            shape = (row_count, per_group, col_width, chunk)
            rights.append(exchange(right.astype(jnp.bfloat16).reshape(shape)))
            lefts.append(exchange(left.astype(jnp.bfloat16).reshape(shape)))
            gates.append(jax.nn.sigmoid(projected[4 * CH :]))
        following = []
        for values, left, gate in zip(current, lefts, gates):
            merged = exchange(channel_products(left, rights)).reshape(CH, col_width, chunk)
            normed_out = channel_norm(merged.astype(jnp.float32)).astype(jnp.bfloat16)
            update = jnp.einsum(
                "cd,cwi->dwi", out_weight[layer_idx], normed_out, preferred_element_type=jnp.float32
            )
            following.append((values.astype(jnp.float32) + gate * update).astype(jnp.bfloat16))
        current = following
    template_count = lax.axis_size("tmpl")
    results = []
    for values in current:
        normed_final = channel_norm(values.astype(jnp.float32))
        summed = lax.psum(normed_final.astype(jnp.bfloat16), "tmpl").astype(jnp.float32)
        hidden = jnp.maximum(summed / template_count, 0.0).astype(jnp.bfloat16)
        results.append(
            jnp.einsum("cz,cwi->zwi", final_weight, hidden, preferred_element_type=jnp.float32)
            .astype(jnp.bfloat16)
        )
    return jnp.concatenate(results, axis=2)


def on_device(pair_maps, crop_tiles, full_length, proj_weight, out_weight, final_weight):
    row_count = lax.axis_size("row")
    my_index = lax.axis_index("row")
    pair_local = pair_maps[0]
    crop_ids = crop_tiles[0]
    local_rows = pair_local.shape[0]
    col_width = CROP // row_count
    parts_count = max(1, row_count // CH)
    per_group = CH * parts_count // row_count
    groups = CH // per_group
    part_rows = CROP // parts_count
    steps_crop = jnp.arange(CROP, dtype=jnp.int32)
    position = crop_ids[steps_crop // TILE] * TILE + steps_crop % TILE
    usable = (position < full_length[0]).astype(jnp.float32)
    col_usable = lax.dynamic_slice_in_dim(usable, my_index * col_width, col_width)
    pair_mask = col_usable[:, None] * usable[None, :]
    columns = pair_local.reshape(local_rows, FULL // TILE, TILE, CH)[:, crop_ids]
    columns = columns.reshape(local_rows, CROP * CH)
    received = lax.all_to_all(columns, "row", split_axis=1, concat_axis=0, tiled=True)
    cropped = received.reshape(FULL // TILE, TILE, col_width * CH)[crop_ids]
    current = jnp.transpose(cropped.reshape(CROP, col_width, CH), (2, 1, 0))
    for layer_idx in range(NLAYER):
        normed_in = channel_norm(current.astype(jnp.float32)).astype(jnp.bfloat16)
        projected = jnp.einsum(
            "cd,cwi->dwi", proj_weight[layer_idx], normed_in, preferred_element_type=jnp.float32
        )
        left_proj = (jax.nn.sigmoid(projected[:CH]) * projected[CH : 2 * CH] * pair_mask).astype(
            jnp.bfloat16
        )
        right_proj = (
            jax.nn.sigmoid(projected[2 * CH : 3 * CH]) * projected[3 * CH : 4 * CH] * pair_mask
        ).astype(jnp.bfloat16)
        gate_vals = jax.nn.sigmoid(projected[4 * CH :])
        left_send = left_proj.reshape(groups, per_group, col_width, parts_count, part_rows)
        left_send = jnp.transpose(left_send, (0, 3, 1, 2, 4)).reshape(
            row_count, per_group, col_width, part_rows
        )
        right_send = right_proj.reshape(groups, per_group, col_width, parts_count, part_rows)
        right_send = jnp.transpose(right_send, (0, 3, 1, 2, 4)).reshape(
            row_count, per_group, col_width, part_rows
        )
        left_got, right_got = (
            lax.all_to_all(left_send, "row", split_axis=0, concat_axis=2, tiled=True),
            lax.all_to_all(right_send, "row", split_axis=0, concat_axis=2, tiled=True),
        )
        right_whole = right_got[0]
        for bit_pos in range(parts_count.bit_length() - 1):
            partner = from_partner(right_whole, "row", bit_pos)
            lower_side = my_index // (1 << bit_pos) % 2 == 0
            right_whole = jnp.where(
                lower_side,
                jnp.concatenate([right_whole, partner], axis=2),
                jnp.concatenate([partner, right_whole], axis=2),
            )
        products = jnp.einsum(
            "cki,ckj->cij", left_got[0], right_whole, preferred_element_type=jnp.float32
        ).astype(jnp.bfloat16)
        back_send = jnp.transpose(
            products.reshape(per_group, part_rows, row_count, col_width), (2, 0, 3, 1)
        )
        back_got = lax.all_to_all(back_send, "row", split_axis=0, concat_axis=0, tiled=True)
        merged = back_got.reshape(groups, parts_count, per_group, col_width, part_rows)
        merged = jnp.transpose(merged, (0, 2, 3, 1, 4)).reshape(CH, col_width, CROP)
        normed_out = channel_norm(merged.astype(jnp.float32)).astype(jnp.bfloat16)
        update = jnp.einsum(
            "cd,cwi->dwi", out_weight[layer_idx], normed_out, preferred_element_type=jnp.float32
        )
        current = (current.astype(jnp.float32) + gate_vals * update).astype(jnp.bfloat16)
    normed_final = channel_norm(current.astype(jnp.float32))
    template_count = lax.axis_size("tmpl")
    summed = lax.psum(normed_final.astype(jnp.bfloat16), "tmpl").astype(jnp.float32)
    hidden = jnp.maximum(summed / template_count, 0.0).astype(jnp.bfloat16)
    result = jnp.einsum(
        "cz,cwi->zwi", final_weight, hidden, preferred_element_type=jnp.float32
    ).astype(jnp.bfloat16)
    return result


def solution(mesh):
    placed = (P("tmpl", "row", None, None), P("tmpl", None), P(), P(), P(), P())
    rows = mesh.shape["row"]
    whole_tiles = FULL // rows == TILE and CH % rows == 0
    return jax.shard_map(
        in_chunks if whole_tiles else on_device,
        mesh=mesh,
        in_specs=placed,
        out_specs=P(None, "row", None),
        check_vma=False,
    )
```

```python
import jax
import jax.numpy as jnp
from jax import lax
from jax.experimental import pallas as pl
from jax.experimental.pallas import tpu as pltpu
from jax.sharding import PartitionSpec as P

CH = 64
CROP = 1024
TILE = 128
NLAYER = 2
FULL = 2048


EPSILON = 1e-05


def from_partner(value, axis, bit):
    mask = 2**bit
    pairs = [(source, source ^ mask) for source in range(lax.axis_size(axis))]
    return lax.ppermute(value, axis, pairs)


def channel_norm(values):
    center = values - jnp.mean(values, axis=0, keepdims=True)
    spread = jnp.mean(center * center, axis=0, keepdims=True)
    return center * lax.rsqrt(spread + EPSILON)


SPLIT = 2


def product_kernel(left_ref, *refs):
    rights, out_ref = refs[:-1], refs[-1]
    sources, _, width, chunk = left_ref.shape
    left = left_ref[...].reshape(sources * width, chunk)
    per = out_ref.shape[0] // len(rights)
    for number, right_ref in enumerate(rights):
        right = right_ref[...].reshape(sources * width, right_ref.shape[-1])
        product = lax.dot_general(
            right, left, (((0,), (0,)), ((), ())), preferred_element_type=jnp.float32
        )
        out_ref[number * per : (number + 1) * per] = product.astype(out_ref.dtype).reshape(
            per, 1, width, chunk
        )


def channel_products(left, rights):
    sources, channels, width, chunk = left.shape
    spec = pl.BlockSpec((sources, 1, width, chunk), lambda c: (0, c, 0, 0))
    depth = sources * width
    return pl.pallas_call(
        product_kernel,
        grid=(channels,),
        in_specs=[spec] * (1 + len(rights)),
        out_specs=spec,
        out_shape=jax.ShapeDtypeStruct(left.shape, left.dtype),
        compiler_params=pltpu.CompilerParams(vmem_limit_bytes=32 << 20),
        cost_estimate=pl.CostEstimate(
            flops=2 * channels * depth * depth * chunk,
            bytes_accessed=2 * left.size * (2 + len(rights)),
            transcendentals=0,
        ),
    )(left, *rights)


def exchange(value):
    return lax.all_to_all(value, "row", split_axis=0, concat_axis=0, tiled=True)


def template_sum(values):
    template_count = lax.axis_size("tmpl")
    passing = channel_norm(values.astype(jnp.float32)).astype(jnp.bfloat16)
    terms = [passing]
    for _ in range(template_count - 1):
        ring = [(source, (source + 1) % template_count) for source in range(template_count)]
        passing = lax.ppermute(passing, "tmpl", ring)
        terms.append(passing)
    return sum(term.astype(jnp.float32) for term in terms)


def in_chunks(pair_maps, crop_tiles, full_length, proj_weight, out_weight, final_weight):
    row_count = lax.axis_size("row")
    my_index = lax.axis_index("row")
    crop_ids = crop_tiles[0]
    col_width = CROP // row_count
    per_group = CH // row_count
    tiles = CROP // TILE
    chunk = CROP // SPLIT
    steps_crop = jnp.arange(CROP, dtype=jnp.int32)
    position = crop_ids[steps_crop // TILE] * TILE + steps_crop % TILE
    usable = (position < full_length[0]).astype(jnp.float32)
    col_usable = lax.dynamic_slice_in_dim(usable, my_index * col_width, col_width)
    pair_mask = col_usable[:, None] * usable[None, :]
    masks = jnp.split(pair_mask, SPLIT, axis=1)
    by_channel = jnp.transpose(pair_maps[0], (0, 2, 1))
    columns = jnp.concatenate(
        [
            lax.dynamic_slice_in_dim(by_channel, crop_ids[tile] * TILE, TILE, axis=2)
            for tile in range(tiles)
        ],
        axis=2,
    )
    send = jnp.transpose(columns, (2, 1, 0)).reshape(row_count, col_width, CH, TILE)
    got = exchange(send)
    per = tiles // SPLIT
    current = []
    for number in range(SPLIT):
        pieces = [
            lax.dynamic_index_in_dim(got, crop_ids[number * per + tile], 0, keepdims=False)
            for tile in range(per)
        ]
        current.append(jnp.transpose(jnp.concatenate(pieces, axis=2), (1, 0, 2)))
    for layer_idx in range(NLAYER):
        lefts, rights, gates = [], [], []
        for values, mask in zip(current, masks):
            normed_in = channel_norm(values.astype(jnp.float32)).astype(jnp.bfloat16)
            projected = jnp.einsum(
                "cd,cwi->dwi", proj_weight[layer_idx], normed_in, preferred_element_type=jnp.float32
            )
            left = jax.nn.sigmoid(projected[:CH]) * projected[CH : 2 * CH] * mask
            right = jax.nn.sigmoid(projected[2 * CH : 3 * CH]) * projected[3 * CH : 4 * CH] * mask
            shape = (row_count, per_group, col_width, chunk)
            rights.append(exchange(right.astype(jnp.bfloat16).reshape(shape)))
            lefts.append(exchange(left.astype(jnp.bfloat16).reshape(shape)))
            gates.append(jax.nn.sigmoid(projected[4 * CH :]))
        following, summed = [], []
        for values, left, gate in zip(current, lefts, gates):
            merged = exchange(channel_products(left, rights)).reshape(CH, col_width, chunk)
            if summed:
                merged, summed[-1] = lax.optimization_barrier((merged, summed[-1]))
            normed_out = channel_norm(merged.astype(jnp.float32)).astype(jnp.bfloat16)
            update = jnp.einsum(
                "cd,cwi->dwi", out_weight[layer_idx], normed_out, preferred_element_type=jnp.float32
            )
            following.append((values.astype(jnp.float32) + gate * update).astype(jnp.bfloat16))
            if layer_idx == NLAYER - 1:
                summed.append(template_sum(following[-1]))
        current = following
    template_count = lax.axis_size("tmpl")
    results = []
    for total in summed:
        hidden = jnp.maximum(total / template_count, 0.0).astype(jnp.bfloat16)
        results.append(
            jnp.einsum("cz,cwi->zwi", final_weight, hidden, preferred_element_type=jnp.float32)
            .astype(jnp.bfloat16)
        )
    return jnp.concatenate(results, axis=2)


def on_device(pair_maps, crop_tiles, full_length, proj_weight, out_weight, final_weight):
    row_count = lax.axis_size("row")
    my_index = lax.axis_index("row")
    pair_local = pair_maps[0]
    crop_ids = crop_tiles[0]
    local_rows = pair_local.shape[0]
    col_width = CROP // row_count
    parts_count = max(1, row_count // CH)
    per_group = CH * parts_count // row_count
    groups = CH // per_group
    part_rows = CROP // parts_count
    steps_crop = jnp.arange(CROP, dtype=jnp.int32)
    position = crop_ids[steps_crop // TILE] * TILE + steps_crop % TILE
    usable = (position < full_length[0]).astype(jnp.float32)
    col_usable = lax.dynamic_slice_in_dim(usable, my_index * col_width, col_width)
    pair_mask = col_usable[:, None] * usable[None, :]
    columns = pair_local.reshape(local_rows, FULL // TILE, TILE, CH)[:, crop_ids]
    columns = columns.reshape(local_rows, CROP * CH)
    received = lax.all_to_all(columns, "row", split_axis=1, concat_axis=0, tiled=True)
    cropped = received.reshape(FULL // TILE, TILE, col_width * CH)[crop_ids]
    current = jnp.transpose(cropped.reshape(CROP, col_width, CH), (2, 1, 0))
    for layer_idx in range(NLAYER):
        normed_in = channel_norm(current.astype(jnp.float32)).astype(jnp.bfloat16)
        projected = jnp.einsum(
            "cd,cwi->dwi", proj_weight[layer_idx], normed_in, preferred_element_type=jnp.float32
        )
        left_proj = (jax.nn.sigmoid(projected[:CH]) * projected[CH : 2 * CH] * pair_mask).astype(
            jnp.bfloat16
        )
        right_proj = (
            jax.nn.sigmoid(projected[2 * CH : 3 * CH]) * projected[3 * CH : 4 * CH] * pair_mask
        ).astype(jnp.bfloat16)
        gate_vals = jax.nn.sigmoid(projected[4 * CH :])
        left_send = left_proj.reshape(groups, per_group, col_width, parts_count, part_rows)
        left_send = jnp.transpose(left_send, (0, 3, 1, 2, 4)).reshape(
            row_count, per_group, col_width, part_rows
        )
        right_send = right_proj.reshape(groups, per_group, col_width, parts_count, part_rows)
        right_send = jnp.transpose(right_send, (0, 3, 1, 2, 4)).reshape(
            row_count, per_group, col_width, part_rows
        )
        left_got, right_got = (
            lax.all_to_all(left_send, "row", split_axis=0, concat_axis=2, tiled=True),
            lax.all_to_all(right_send, "row", split_axis=0, concat_axis=2, tiled=True),
        )
        right_whole = right_got[0]
        for bit_pos in range(parts_count.bit_length() - 1):
            partner = from_partner(right_whole, "row", bit_pos)
            lower_side = my_index // (1 << bit_pos) % 2 == 0
            right_whole = jnp.where(
                lower_side,
                jnp.concatenate([right_whole, partner], axis=2),
                jnp.concatenate([partner, right_whole], axis=2),
            )
        products = jnp.einsum(
            "cki,ckj->cij", left_got[0], right_whole, preferred_element_type=jnp.float32
        ).astype(jnp.bfloat16)
        back_send = jnp.transpose(
            products.reshape(per_group, part_rows, row_count, col_width), (2, 0, 3, 1)
        )
        back_got = lax.all_to_all(back_send, "row", split_axis=0, concat_axis=0, tiled=True)
        merged = back_got.reshape(groups, parts_count, per_group, col_width, part_rows)
        merged = jnp.transpose(merged, (0, 2, 3, 1, 4)).reshape(CH, col_width, CROP)
        normed_out = channel_norm(merged.astype(jnp.float32)).astype(jnp.bfloat16)
        update = jnp.einsum(
            "cd,cwi->dwi", out_weight[layer_idx], normed_out, preferred_element_type=jnp.float32
        )
        current = (current.astype(jnp.float32) + gate_vals * update).astype(jnp.bfloat16)
    normed_final = channel_norm(current.astype(jnp.float32))
    template_count = lax.axis_size("tmpl")
    summed = lax.psum(normed_final.astype(jnp.bfloat16), "tmpl").astype(jnp.float32)
    hidden = jnp.maximum(summed / template_count, 0.0).astype(jnp.bfloat16)
    result = jnp.einsum(
        "cz,cwi->zwi", final_weight, hidden, preferred_element_type=jnp.float32
    ).astype(jnp.bfloat16)
    return result


def solution(mesh):
    placed = (P("tmpl", "row", None, None), P("tmpl", None), P(), P(), P(), P())
    rows = mesh.shape["row"]
    whole_tiles = FULL // rows == TILE and CH % rows == 0
    return jax.shard_map(
        in_chunks if whole_tiles else on_device,
        mesh=mesh,
        in_specs=placed,
        out_specs=P(None, "row", None),
        check_vma=False,
    )
```
